32 devices in a mesh: seq: 4 (over x, core), head: 8 (over z, y).
Axes of the slice: x: 2, y: 2, z: 4, core: 2. Of those that a mesh axis runs over, the one named last changes fastest.
Arguments:
- features: bfloat16 [16384, 12288], P(('seq', 'head')), may hold values from -6 to 6
- selector: bfloat16 [16384, 256], P(('seq', 'head')), may hold values from -6 to 6
- step_input: bfloat16 [16384, 96], P(('seq', 'head')), may hold values from -2 to 20
- feature_kernel: float32 [4, 12288], replicated, may hold values from -3 to 3
- selector_kernel: float32 [4, 256], replicated, may hold values from -3 to 3
- feature_offset: float32 [12288], replicated, may hold values from -3 to 3
- selector_offset: float32 [256], replicated, may hold values from -3 to 3
- decay_log: float32 [96], replicated, may hold values from -2.4 to 0.1
- step_offset: float32 [96], replicated, may hold values from -12 to -2
- skip_scale: float32 [96], replicated, may hold values from 0.5 to 1.5
- norm_gain: float32 [12288], replicated, may hold values from 0.5 to 1.5
Outputs:
- output: bfloat16 [16384, 12288], P(('seq', 'head'))
The draws below stay inside these ranges and needn't reach their ends.
All inputs are finite; a program needn't handle non-finite values.
Results may differ from the reference program's by a relative error of at most 0.008.
Values may be sent and summed in bfloat16 or wider, within the bound.
No kernel may reach another device: no remote copies, remote signals or barrier semaphores. Data moves between devices by JAX's collectives and lax.ppermute only.
A program may use at most 192 MiB of HBM per device.

```python
import jax
import jax.numpy as jnp
from jax import lax

HEADS = 96
HEAD_DIM = 128
STATE = 128
KERNEL = 4
SPAN = 256
TOKEN_COUNT = 16384


def head_rates(key):
    classes = jax.random.randint(jax.random.fold_in(key, 11), (HEADS,), 0, 8)
    quick = classes < 4
    unit = jax.random.uniform(jax.random.fold_in(key, 12), (HEADS,), jnp.float32)
    spread = jax.random.uniform(jax.random.fold_in(key, 13), (HEADS,), jnp.float32)
    rate_quick = jnp.exp(jnp.log(0.3) + unit * (jnp.log(1.0) - jnp.log(0.3)))
    rate_slow = jnp.exp(jnp.log(0.1) + unit * (jnp.log(0.2) - jnp.log(0.1)))
    rate = jnp.where(quick, rate_quick, rate_slow)
    target_quick = (1.0 / 50.0 + spread * (1.0 / 30.0 - 1.0 / 50.0)) / rate
    target_slow = (0.4 + 0.4 * spread) / (rate * TOKEN_COUNT)
    target = jnp.where(quick, target_quick, target_slow)
    return (jnp.log(rate), jnp.log(jnp.expm1(target)))


def draw_decay_log(key, part):
    return head_rates(key)[0]


def draw_step_offset(key, part):
    return head_rates(key)[1]


def draw_step_input(key, part):
    rates, offset = head_rates(key)
    random_jitter = jnp.clip(0.5 * jax.random.normal(jax.random.fold_in(key, 21), (TOKEN_COUNT, HEADS), jnp.float32), -2.0, 2.0)
    locations = jax.random.randint(jax.random.fold_in(key, 22), (4,), 0, TOKEN_COUNT)
    sudden_spike = jnp.any(jnp.arange(TOKEN_COUNT)[:, None] == locations[None, :], axis=1)
    target = jax.random.uniform(jax.random.fold_in(key, 23), (TOKEN_COUNT, HEADS), jnp.float32, 1.5, 3.0)
    raised_values = jnp.log(jnp.expm1(target)) - offset[None, :]
    return jnp.where(sudden_spike[:, None], raised_values, random_jitter).astype(jnp.bfloat16)


def block_levels(own_key, extent, pieces, least, high):
    def one(axis_at, parts):
        steps = jax.random.uniform(jax.random.fold_in(jax.random.fold_in(own_key, 6), axis_at), (parts,), jnp.float32, least / len(pieces), high / len(pieces))
        return jnp.repeat(jnp.exp(steps), extent[axis_at] // parts).reshape((-1,) + (1,) * (len(extent) - axis_at - 1))

    level = one(*pieces[0])
    for cut in pieces[1:]:
        level = level * one(*cut)
    return level


def gaussian(rng, shape, scale, most, split=(), held_as=jnp.bfloat16):
    level = block_levels(rng, shape, split, -0.22, 0.18) if split else 1.0
    drawn = jax.random.normal(rng, shape, jnp.float32) * scale * level
    return jnp.minimum(jnp.maximum(drawn, -most), most).astype(held_as)


def setup_inputs(seed: int = 0) -> dict:
    key_list = jax.random.split(jax.random.key(seed), 12)
    return {
        "features": gaussian(key_list[0], (TOKEN_COUNT, HEADS * HEAD_DIM), 1.0, 6.0, ((0, 32),)),
        "selector": gaussian(key_list[1], (TOKEN_COUNT, 2 * STATE), 1.0, 6.0, ((0, 32),)),
        "step_input": draw_step_input(jax.random.fold_in(key_list[11], 71), 0),
        "feature_kernel": gaussian(key_list[3], (KERNEL, HEADS * HEAD_DIM), KERNEL ** -0.5, 3.0, (), jnp.float32),
        "selector_kernel": gaussian(key_list[4], (KERNEL, 2 * STATE), KERNEL ** -0.5, 3.0, (), jnp.float32),
        "feature_offset": gaussian(key_list[5], (HEADS * HEAD_DIM,), 0.5, 3.0, (), jnp.float32),
        "selector_offset": gaussian(key_list[6], (2 * STATE,), 0.5, 3.0, (), jnp.float32),
        "decay_log": draw_decay_log(jax.random.fold_in(key_list[11], 71), 0),
        "step_offset": draw_step_offset(jax.random.fold_in(key_list[11], 71), 0),
        "skip_scale": jnp.clip(jax.random.uniform(key_list[9], (HEADS,), jnp.float32, 0.5, 1.5), 0.5, 1.5),
        "norm_gain": jnp.clip(1.0 + 0.1 * jax.random.normal(key_list[10], (HEADS * HEAD_DIM,), jnp.float32), 0.5, 1.5),
    }


def round_trip(values):
    return lax.optimization_barrier(values.astype(jnp.bfloat16)).astype(jnp.float32)

def causal_filter(tail_rows, new_rows, kernel, offset):
    length = new_rows.shape[0]
    window = jnp.concatenate([tail_rows, new_rows], axis=0).astype(jnp.float32)
    summed = jnp.broadcast_to(offset[None, :], (length, offset.shape[0]))
    for delay_step in range(kernel.shape[0]):
        summed = summed + kernel[delay_step][None, :] * window[delay_step:delay_step + length]
    return jax.nn.silu(summed).astype(jnp.bfloat16)

def span_terms(feature_matrix_rows, write_rows, read_rows, step_size, log_decay):
    length = feature_matrix_rows.shape[0]
    head_count = step_size.shape[1]
    head_view = feature_matrix_rows.reshape(length, head_count, -1).astype(jnp.float32)
    cumulative = jnp.cumsum(log_decay, axis=0)
    inputs = round_trip(step_size[:, :, None] * head_view)
    scores = jnp.dot(read_rows, write_rows.T, preferred_element_type=jnp.float32)
    log_spacing = cumulative.T[:, :, None] - cumulative.T[:, None, :]
    causal = jnp.arange(length)[:, None] >= jnp.arange(length)[None, :]
    decay_mask = jnp.exp(jnp.where(causal[None], log_spacing, -jnp.inf))
    mixing = round_trip(scores[None] * decay_mask)
    diagonal = jnp.einsum('hij,jhp->ihp', mixing, inputs)
    log_total = cumulative[-1]
    weighted = round_trip((step_size * jnp.exp(log_total[None, :] - cumulative))[:, :, None] * head_view)
    span_state = jnp.einsum('jn,jhp->hnp', write_rows.astype(jnp.float32), weighted)
    return (diagonal, cumulative, span_state, log_total)

def span_output(diagonal, cumulative, read_rows, entry_state, feature_matrix_rows, skip_scale):
    length, head_count, head_width = diagonal.shape
    carried = jnp.einsum('in,hnp->ihp', read_rows.astype(jnp.float32), round_trip(entry_state))
    head_view = feature_matrix_rows.reshape(length, head_count, head_width).astype(jnp.float32)
    summed = diagonal + jnp.exp(cumulative)[:, :, None] * carried + skip_scale[None, :, None] * head_view
    return summed.reshape(length, head_count * head_width).astype(jnp.bfloat16)

def normalize(values, norm_gain):
    widened = values.astype(jnp.float32)
    square = lax.optimization_barrier(jnp.mean(widened * widened, axis=-1, keepdims=True))
    return (widened * lax.rsqrt(square + 1e-05) * norm_gain[None, :]).astype(jnp.bfloat16)

def reference(features, selector, step_input, feature_kernel, selector_kernel, feature_offset, selector_offset, decay_log, step_offset, skip_scale, norm_gain):
    span_count = TOKEN_COUNT // SPAN
    channels = HEADS * HEAD_DIM
    tail_count = KERNEL - 1

    def advance(carry_state, record):
        entry_state, feature_tail, selector_tail = carry_state
        feature_matrix_rows, selector_rows, step_rows = record
        feature_conv = causal_filter(feature_tail, feature_matrix_rows, feature_kernel, feature_offset)
        selector_conv = causal_filter(selector_tail, selector_rows, selector_kernel, selector_offset)
        write_rows = selector_conv[:, :STATE]
        read_rows = selector_conv[:, STATE:]
        step_size = jax.nn.softplus(step_rows.astype(jnp.float32) + step_offset[None, :])
        log_decay = -jnp.exp(decay_log)[None, :] * step_size
        diagonal, cumulative, span_state, log_total = span_terms(feature_conv, write_rows, read_rows, step_size, log_decay)
        mixed = span_output(diagonal, cumulative, read_rows, entry_state, feature_conv, skip_scale)
        normed = normalize(mixed, norm_gain)
        next_state = jnp.exp(log_total)[:, None, None] * entry_state + span_state
        return ((next_state, feature_matrix_rows[SPAN - tail_count:], selector_rows[SPAN - tail_count:]), normed)
    initial = (jnp.zeros((HEADS, STATE, HEAD_DIM), jnp.float32), jnp.zeros((tail_count, channels), jnp.bfloat16), jnp.zeros((tail_count, 2 * STATE), jnp.bfloat16))
    records = (features.reshape(span_count, SPAN, channels), selector.reshape(span_count, SPAN, 2 * STATE), step_input.reshape(span_count, SPAN, HEADS))
    final_carry, outputs = lax.scan(advance, initial, records)
    return outputs.reshape(TOKEN_COUNT, channels)
```

```python
import functools

import jax
import jax.numpy as jnp
from jax import lax
from jax.experimental import pallas as pl
from jax.experimental.pallas import tpu as pltpu
from jax.sharding import Mesh, PartitionSpec as P

SPAN = 256
LANES = 128
LOG2E = 1.4426950408889634
BF16 = jnp.bfloat16
F32 = jnp.float32
SMEM = pltpu.MemorySpace.SMEM
VMEM = pltpu.MemorySpace.VMEM
ALL = ("seq", "pair", "side")
GROUP = ("seq", "pair")


def dot(a, b):
    return jnp.dot(a, b, preferred_element_type=F32)


def cost(flops, nbytes):
    return pl.CostEstimate(flops=int(flops), bytes_accessed=int(nbytes), transcendentals=0)


def whole_vmem(n):
    return [pl.BlockSpec(memory_space=VMEM)] * n


def rates_kernel(step_ref, off_ref, dlog_ref, dt_ref, wst_ref, cum_ref, cumt_ref, ecum_ref, edev_ref, tot_ref, last_ref):
    rows, heads = step_ref.shape
    spans = rows // SPAN
    for ref in (dt_ref, wst_ref, cum_ref, ecum_ref, edev_ref):
        ref[...] = jnp.zeros_like(ref)
    raw = step_ref[...].astype(F32) + off_ref[...]
    step = jnp.maximum(raw, 0.0) + jnp.log1p(jnp.exp(-jnp.abs(raw)))
    decay = step * (-LOG2E * jnp.exp(dlog_ref[...]))
    at = lax.broadcasted_iota(jnp.int32, (SPAN, SPAN), 0)
    by = lax.broadcasted_iota(jnp.int32, (SPAN, SPAN), 1)
    tri = (at >= by).astype(F32)
    before = jnp.zeros((1, heads), F32)
    last = jnp.zeros((1, heads), F32)
    for s in range(spans):
        at_rows = pl.ds(s * SPAN, SPAN)
        piece = decay[s * SPAN : (s + 1) * SPAN]
        cum = jnp.dot(tri, piece, precision=lax.Precision.HIGHEST, preferred_element_type=F32)
        total = cum[SPAN - 1 : SPAN]
        own = step[s * SPAN : (s + 1) * SPAN]
        dt_ref[at_rows, :heads] = own
        wst_ref[at_rows, :heads] = own * jnp.exp2(total - cum)
        cum_ref[at_rows, :heads] = cum
        ecum_ref[at_rows, :heads] = jnp.exp2(cum)
        edev_ref[at_rows, :heads] = jnp.exp2(cum + before)
        before = before + total
        last = total
    cumt_ref[...] = jnp.transpose(cum_ref[...])
    tot_ref[...] = before
    last_ref[...] = jnp.exp2(last)


def rates(step_input, step_offset, decay_log):
    rows, heads = step_input.shape
    wide = jax.ShapeDtypeStruct((rows, LANES), F32)
    row = jax.ShapeDtypeStruct((1, heads), F32)
    return pl.pallas_call(
        rates_kernel,
        out_shape=(wide, wide, wide, jax.ShapeDtypeStruct((LANES, rows), F32), wide, wide, row, row),
        in_specs=whole_vmem(3),
        out_specs=whole_vmem(8),
        cost_estimate=cost(1e9, 2e6),
        name="rates",
    )(step_input, step_offset[None, :], decay_log[None, :])


def filtered(source, taps, offset, length):
    total = offset
    for k in range(taps.shape[0]):
        total = total + taps[k : k + 1] * source(k, length)
    return (total + total * jnp.tanh(total)).astype(BF16)


def selector_kernel(sel_ref, tail_ref, taps_ref, off_ref, write_ref, read_ref, scores_ref, buf_ref):
    rows, width = sel_ref.shape
    count = tail_ref.shape[0]
    size = width // 2
    buf_ref[8 - count : 8, :] = tail_ref[...].astype(F32)
    buf_ref[8 : 8 + rows, :] = sel_ref[...].astype(F32)
    out = filtered(
        lambda k, length: buf_ref[8 - count + k : 8 - count + k + length, :],
        0.5 * taps_ref[...], 0.5 * off_ref[...], rows)
    write_ref[...] = jnp.transpose(out[:, :size].astype(F32)).astype(BF16)
    read_ref[...] = out[:, size:]
    at = lax.broadcasted_iota(jnp.int32, (SPAN, SPAN), 0)
    by = lax.broadcasted_iota(jnp.int32, (SPAN, SPAN), 1)
    for s in range(rows // SPAN):
        at_rows = pl.ds(s * SPAN, SPAN)
        got = dot(read_ref[at_rows, :], write_ref[:, s * SPAN : (s + 1) * SPAN])
        scores_ref[at_rows, :] = jnp.where(at >= by, got, 0.0)


def selectors(selector, tail, taps, offset):
    rows, width = selector.shape
    return pl.pallas_call(
        selector_kernel,
        out_shape=(
            jax.ShapeDtypeStruct((width // 2, rows), BF16),
            jax.ShapeDtypeStruct((rows, width // 2), BF16),
            jax.ShapeDtypeStruct((rows, SPAN), F32),
        ),
        in_specs=whole_vmem(4),
        out_specs=whole_vmem(3),
        scratch_shapes=[pltpu.VMEM((rows + 8, width), F32)],
        cost_estimate=cost(1e8, 2e6),
        name="selectors",
    )(selector, tail, taps, offset[None, :])


def states_kernel(group, start_ref, last_ref, x_ref, tail_ref, taps_ref, off_ref, wst_ref, write_ref,
                  conv_ref, local_ref, first_ref, buf_ref, weighted_ref):
    rows = x_ref.shape[0]
    count = tail_ref.shape[0]
    tile = 64
    head0 = (start_ref[0] + pl.program_id(0)) * group
    factors = pltpu.roll(wst_ref[...], LANES - head0, 1)
    for h in range(group):
        cols = slice(h * LANES, (h + 1) * LANES)
        buf_ref[h, 8 - count : 8, :] = tail_ref[:, cols].astype(F32)
        buf_ref[h, 8 : 8 + rows, :] = x_ref[:, cols].astype(F32)
        taps = 0.5 * taps_ref[:, cols]
        offset = 0.5 * off_ref[:, cols]
        for r in range(0, rows, tile):
            conv = filtered(
                lambda k, length: buf_ref[h, 8 - count + k + r : 8 - count + k + r + length, :],
                taps, offset, tile)
            conv_ref[r : r + tile, cols] = conv
            weighted_ref[r : r + tile, cols] = (
                factors[r : r + tile, h : h + 1] * conv.astype(F32)).astype(BF16)
    spans = rows // SPAN
    for h in range(0, group, 2):
        cols = slice(h * LANES, (h + 2) * LANES)
        got = [dot(write_ref[:, s * SPAN : (s + 1) * SPAN], weighted_ref[s * SPAN : (s + 1) * SPAN, cols])
               for s in range(spans)]
        for j in range(2):
            at_rows = slice((h + j) * LANES, (h + j + 1) * LANES)
            half = slice(j * LANES, (j + 1) * LANES)
            first = got[0][:, half]
            first_ref[at_rows, :] = first.astype(BF16)
            local_ref[at_rows, :] = (got[1][:, half] + last_ref[0, head0 + h + j] * first).astype(BF16)


def states(start, last, features, tail, taps, offset, wst, write, heads, group):
    rows = features.shape[0]
    count = tail.shape[0]
    steps = heads // group
    width = group * LANES
    spec = pltpu.PrefetchScalarGridSpec(
        num_scalar_prefetch=1,
        grid=(steps,),
        in_specs=[
            pl.BlockSpec(memory_space=SMEM),
            pl.BlockSpec((rows, width), lambda i, s: (0, s[0] + i)),
            pl.BlockSpec((count, width), lambda i, s: (0, s[0] + i)),
            pl.BlockSpec((taps.shape[0], width), lambda i, s: (0, s[0] + i)),
            pl.BlockSpec((1, width), lambda i, s: (0, s[0] + i)),
            pl.BlockSpec((rows, LANES), lambda i, s: (0, 0)),
            pl.BlockSpec(write.shape, lambda i, s: (0, 0)),
        ],
        out_specs=[
            pl.BlockSpec((rows, width), lambda i, s: (0, i)),
            pl.BlockSpec((width, LANES), lambda i, s: (i, 0)),
            pl.BlockSpec((width, LANES), lambda i, s: (i, 0)),
        ],
        scratch_shapes=[pltpu.VMEM((group, rows + 8, LANES), F32), pltpu.VMEM((rows, width), BF16)],
    )
    size = heads * LANES
    return pl.pallas_call(
        functools.partial(states_kernel, group),
        out_shape=(
            jax.ShapeDtypeStruct((rows, size), BF16),
            jax.ShapeDtypeStruct((size, LANES), BF16),
            jax.ShapeDtypeStruct((size, LANES), BF16),
        ),
        grid_spec=spec,
        cost_estimate=cost(heads * 20e6, 4 * rows * size),
        name="states",
    )(start, last, features, tail, taps, offset[None, :], wst, write)


def inner_kernel(group, start_ref, skip_ref, conv_ref, first_ref, dt_ref, cum_ref, ecum_ref, cumt_ref, scores_ref, read_ref, out_ref):
    rows = conv_ref.shape[0]
    half = SPAN // 2
    head0 = (start_ref[0] + pl.program_id(0)) * group
    shift = LANES - head0
    steps = pltpu.roll(dt_ref[...], shift, 1)
    cums = pltpu.roll(cum_ref[...], shift, 1)
    ecums = pltpu.roll(ecum_ref[...], shift, 1)
    for h in range(group):
        cols = slice(h * LANES, (h + 1) * LANES)
        row = cumt_ref[pl.ds(head0 + h, 1), :]
        skip = skip_ref[head0 + h]
        for s in range(rows // SPAN):
            top = slice(s * SPAN, s * SPAN + half)
            low = slice(s * SPAN + half, (s + 1) * SPAN)
            head_view = conv_ref[s * SPAN : (s + 1) * SPAN, cols].astype(F32)
            inputs = (steps[s * SPAN : (s + 1) * SPAN, h : h + 1] * head_view).astype(BF16)
            c_top, c_low = cums[top, h : h + 1], cums[low, h : h + 1]
            r_top, r_low = row[:, top], row[:, low]
            m00 = scores_ref[top, :half] * jnp.exp2(jnp.minimum(c_top - r_top, 0.0))
            m10 = scores_ref[low, :half] * jnp.exp2(c_low - r_top)
            m11 = scores_ref[low, half:] * jnp.exp2(jnp.minimum(c_low - r_low, 0.0))
            bottom = jnp.concatenate([m10.astype(BF16), m11.astype(BF16)], axis=1)
            y_top = dot(m00.astype(BF16), inputs[:half])
            y_low = dot(bottom, inputs)
            if s > 0:
                carried = dot(read_ref[s * SPAN : (s + 1) * SPAN, :], first_ref[cols, :])
                y_top = y_top + ecums[top, h : h + 1] * carried[:half]
                y_low = y_low + ecums[low, h : h + 1] * carried[half:]
            out_ref[top, cols] = (y_top + skip * head_view[:half]).astype(BF16)
            out_ref[low, cols] = (y_low + skip * head_view[half:]).astype(BF16)


def inner(start, skip, conv, first, dt, cum, ecum, cumt, scores, read, group):
    rows, size = conv.shape
    width = group * LANES
    fixed = lambda a: pl.BlockSpec(a.shape, lambda i, s: (0, 0))
    spec = pltpu.PrefetchScalarGridSpec(
        num_scalar_prefetch=1,
        grid=(size // width,),
        in_specs=[
            pl.BlockSpec(memory_space=SMEM),
            pl.BlockSpec((rows, width), lambda i, s: (0, i)),
            pl.BlockSpec((width, LANES), lambda i, s: (i, 0)),
            fixed(dt), fixed(cum), fixed(ecum), fixed(cumt), fixed(scores), fixed(read),
        ],
        out_specs=pl.BlockSpec((rows, width), lambda i, s: (0, i)),
    )
    return pl.pallas_call(
        functools.partial(inner_kernel, group),
        out_shape=jax.ShapeDtypeStruct((rows, size), BF16),
        grid_spec=spec,
        cost_estimate=cost(size // LANES * 50e6, 4 * rows * size),
        name="inner",
    )(start, skip, conv, first, dt, cum, ecum, cumt, scores, read)


def splat(value):
    return jnp.exp2(jnp.full((1, LANES), value, F32))


def pair_kernel(base, ids_ref, logs_ref, own_ref, got_ref, out_ref):
    side, pair = ids_ref[0], ids_ref[1]
    heads = own_ref.shape[0] // LANES
    head0 = base + side * heads

    def one(h, _):
        at_rows = pl.ds(pl.multiple_of(h * LANES, LANES), LANES)
        other = logs_ref[2 * pair + 1 - side, head0 + h]
        grown = splat(other)
        own, got = own_ref[at_rows, :].astype(F32), got_ref[at_rows, :].astype(F32)
        first = jnp.where(side == 0, own, got)
        second = jnp.where(side == 0, got, own)
        later = splat(logs_ref[2 * pair + 1, head0 + h])
        out_ref[at_rows, :] = (later * first + second).astype(BF16)
        return 0

    lax.fori_loop(0, heads, one, 0)


def pair_total(base, ids, logs, own, got):
    return pl.pallas_call(
        functools.partial(pair_kernel, base),
        out_shape=jax.ShapeDtypeStruct(own.shape, BF16),
        in_specs=[pl.BlockSpec(memory_space=SMEM)] * 2 + whole_vmem(2),
        out_specs=pl.BlockSpec(memory_space=VMEM),
        cost_estimate=cost(1e6, own.size * 6),
        name="pair_total",
    )(ids, logs, own, got)


def prefix_kernel(base, half, ids_ref, logs_ref, in_ref, out_ref):
    side, pair = ids_ref[0], ids_ref[1]
    pairs, rows, _ = in_ref.shape
    part = min(rows, LANES)
    for r in range(0, rows, part):
        head = base + side * half + (pair * rows + r) // LANES
        running = jnp.zeros((part, LANES), F32)
        for j in range(pairs):
            out_ref[j, r : r + part, :] = running.astype(BF16)
            grown = splat(logs_ref[2 * j, head] + logs_ref[2 * j + 1, head])
            running = grown * running + in_ref[j, r : r + part, :].astype(F32)


def prefix(base, half, ids, logs, totals):
    return pl.pallas_call(
        functools.partial(prefix_kernel, base, half),
        out_shape=jax.ShapeDtypeStruct(totals.shape, BF16),
        in_specs=[pl.BlockSpec(memory_space=SMEM)] * 2 + whole_vmem(1),
        out_specs=pl.BlockSpec(memory_space=VMEM),
        cost_estimate=cost(1e6, totals.size * 4),
        name="prefix",
    )(ids, logs, totals)


def split_kernel(base, ids_ref, logs_ref, in_ref, own_ref, got_ref, keep_ref, send_ref):
    side, pair = ids_ref[0], ids_ref[1]
    heads = own_ref.shape[0] // LANES
    head0 = base + side * heads

    def one(h, _):
        at_rows = pl.ds(pl.multiple_of(h * LANES, LANES), LANES)
        entering = in_ref[at_rows, :].astype(F32)
        first = jnp.where(side == 0, own_ref[at_rows, :].astype(F32), got_ref[at_rows, :].astype(F32))
        later = splat(logs_ref[2 * pair, head0 + h]) * entering + first
        keep_ref[at_rows, :] = jnp.where(side == 0, entering, later).astype(BF16)
        send_ref[at_rows, :] = jnp.where(side == 0, later, entering).astype(BF16)
        return 0

    lax.fori_loop(0, heads, one, 0)


def split_entering(base, ids, logs, entering, own, got):
    shape = jax.ShapeDtypeStruct(own.shape, BF16)
    return pl.pallas_call(
        functools.partial(split_kernel, base),
        out_shape=(shape, shape),
        in_specs=[pl.BlockSpec(memory_space=SMEM)] * 2 + whole_vmem(3),
        out_specs=whole_vmem(2),
        cost_estimate=cost(1e6, own.size * 10),
        name="split_entering",
    )(ids, logs, entering, own, got)


def finish_kernel(pieces, half, ids_ref, *refs):
    inner_refs, state_refs = refs[:pieces], refs[pieces : 2 * pieces]
    edev_ref, read_ref, gain_ref, out_ref, mixed_ref = refs[2 * pieces :]
    side = ids_ref[0]
    rows = read_ref.shape[0]
    width = half * LANES
    read = read_ref[...]
    square = jnp.zeros((rows, LANES), F32)
    for k in range(pieces):
        head0 = (k // 2) * 2 * half + (side if k % 2 == 0 else 1 - side) * half
        grown = pltpu.roll(edev_ref[...], LANES - head0, 1)
        for h in range(0, half, 2):
            state = jnp.concatenate(
                [state_refs[k][(h + j) * LANES : (h + j + 1) * LANES, :] for j in range(2)], axis=1)
            carried = dot(read, state)
            for j in range(2):
                cols = slice((h + j) * LANES, (h + j + 1) * LANES)
                value = (inner_refs[k][:, cols].astype(F32)
                         + grown[:, h + j : h + j + 1] * carried[:, j * LANES : (j + 1) * LANES])
                value = value.astype(BF16)
                mixed_ref[:, k * width + (h + j) * LANES : k * width + (h + j + 1) * LANES] = value
                value = value.astype(F32)
                square = square + value * value
    mean = jnp.sum(square, axis=1, keepdims=True) * (1.0 / (pieces * width))
    scale = lax.rsqrt(mean + 1e-05)
    for k in range(pieces):
        head0 = (k // 2) * 2 * half + (side if k % 2 == 0 else 1 - side) * half
        col0 = pl.multiple_of(head0 * LANES, LANES)
        for h in range(half):
            value = mixed_ref[:, k * width + h * LANES : k * width + (h + 1) * LANES].astype(F32)
            cols = pl.ds(pl.multiple_of(col0 + h * LANES, LANES), LANES)
            out_ref[:, cols] = (value * scale * gain_ref[:, cols]).astype(BF16)


def finish(ids, inners, entering, edev, read, gain, half):
    rows = read.shape[0]
    pieces = len(inners)
    width = half * LANES
    tile = 64
    spec = pltpu.PrefetchScalarGridSpec(
        num_scalar_prefetch=1,
        grid=(rows // tile,),
        in_specs=[pl.BlockSpec((tile, width), lambda i, s: (i, 0))] * pieces
        + [pl.BlockSpec((width, LANES), lambda i, s: (0, 0))] * pieces
        + [
            pl.BlockSpec((tile, LANES), lambda i, s: (i, 0)),
            pl.BlockSpec((tile, read.shape[1]), lambda i, s: (i, 0)),
            pl.BlockSpec((1, gain.shape[0]), lambda i, s: (0, 0)),
        ],
        out_specs=pl.BlockSpec((tile, gain.shape[0]), lambda i, s: (i, 0)),
        scratch_shapes=[pltpu.VMEM((tile, gain.shape[0]), BF16)],
    )
    return pl.pallas_call(
        functools.partial(finish_kernel, pieces, half),
        out_shape=jax.ShapeDtypeStruct((rows, gain.shape[0]), BF16),
        grid_spec=spec,
        cost_estimate=cost(2e9, 4 * rows * gain.shape[0]),
        name="finish",
    )(ids, *inners, *entering, edev, read, gain[None, :])


def exchanged(block):
    return lax.ppermute(block, "side", [(0, 1), (1, 0)])


def scattered(block, peers):
    return lax.all_to_all(block.reshape(peers, -1, LANES), GROUP, 0, 0)


def on_device(
    features,
    selector,
    step_input,
    feature_kernel,
    selector_kernel,
    feature_offset,
    selector_offset,
    decay_log,
    step_offset,
    skip_scale,
    norm_gain,
):
    rows, channels = features.shape
    heads = decay_log.shape[0]
    tail_count = feature_kernel.shape[0] - 1
    devices = lax.axis_size(ALL)
    peers = lax.axis_size(GROUP)
    side = lax.axis_index("side")
    pair = lax.axis_index(GROUP)
    ids = jnp.stack([side, pair]).astype(jnp.int32)
    chunks = 3
    half = heads // (2 * chunks)
    group = 4

    last_rows = jnp.concatenate([features[rows - tail_count :], selector[rows - tail_count :]], axis=1)
    tail = lax.ppermute(last_rows, ALL, [(i, i + 1) for i in range(devices - 1)])
    dt, wst, cum, cumt, ecum, edev, total, last = rates(step_input, step_offset, decay_log)
    logs = lax.all_to_all(jnp.broadcast_to(total, (devices, heads)), ALL, 0, 0, tiled=True)
    write, read, scores = selectors(selector, tail[:, channels:], selector_kernel, selector_offset)

    convs, firsts, locals_, starts = [], [], [], []
    for c in range(chunks):
        for other in (True, False):
            which = (1 - side) if other else side
            start = ((2 * c + which) * (half // group)).astype(jnp.int32)[None]
            conv, local, first = states(
                start, last, features, tail, feature_kernel, feature_offset, wst, write, half, group)
            convs.append(conv)
            locals_.append(local)
            firsts.append(first)
            starts.append(start)
    inners = [
        inner(starts[k], skip_scale, convs[k], firsts[k], dt, cum, ecum, cumt, scores, read, group)
        for k in range(2 * chunks)
    ]
    pieces, entering = [], []
    for c in range(chunks):
        base = 2 * half * c
        theirs, own = locals_[2 * c], locals_[2 * c + 1]
        got = exchanged(theirs)
        totals = scattered(pair_total(base, ids, logs, own, got), peers)
        entered = scattered(prefix(base, half, ids, logs, totals), peers)
        keep, send = split_entering(base, ids, logs, entered.reshape(own.shape), own, got)
        pieces += [inners[2 * c + 1], inners[2 * c]]
        entering += [keep, exchanged(send)]
    return finish(ids, pieces, entering, edev, read, norm_gain, half)


def solution(mesh):
    devices = mesh.devices
    fine = Mesh(devices.reshape(devices.shape[0], devices.shape[1] // 2, 2), ALL)
    rows = P(ALL, None)
    return jax.shard_map(
        on_device, mesh=fine, in_specs=(rows,) * 3 + (P(),) * 8, out_specs=rows, check_vma=False
    )
```
